512 devices in a mesh: dp: 4 (over y), head: 2 (over core), tile: 64 (over z, x).
Axes of the slice: x: 4, y: 4, z: 16, core: 2. Of those that a mesh axis runs over, the one named last changes fastest.
Arguments:
- tiles_in: bfloat16 [4, 16384, 2560], P('dp', 'tile'), may hold values from -6 to 6
- key_weight: bfloat16 [2560, 1280], P('tile', 'head'), may hold values from -0.125 to 0.125
- value_weight: bfloat16 [2560, 1280], P('tile', 'head'), may hold values from -0.125 to 0.125
- queries: bfloat16 [512, 1280], P(None, 'head'), may hold values from -300 to 300
- out_grad: bfloat16 [4, 512, 1280], P('dp', None, 'head'), may hold values from -1536 to 1536
- valid_count: int32 [4], P('dp'), may hold values from 4096 to 16384, as said below
- tile_mask: int32 [4, 16384], P('dp', 'tile'), may hold values 0 or 1
Outputs:
- tile_grad: bfloat16 [4, 16384, 2560], P('dp', 'tile', 'head')
The draws below stay inside these ranges and needn't reach their ends.
Inputs may be any that keep to these rules, and one draw needn't show every extreme that they name: Some slide has valid_count equal to 16384.
All inputs are finite; a program needn't handle non-finite values. No bound on the sum of `tile_mask` on one device may be relied on, other than what follows from the above.
Results may differ from the reference program's by a relative error of at most 0.022.
Values may be sent and summed in bfloat16 or wider, within the bound.
No kernel may reach another device: no remote copies, remote signals or barrier semaphores. Data moves between devices by JAX's collectives and lax.ppermute only.
A program may use at most 64 MiB of HBM per device.

```python
import jax
import jax.numpy as jnp
from jax import lax

L = 512
HEADS = 16
HDIM = 80
DX = 2560
TILES = 16384
SLIDES = 4
HD = 1280
N_HEAD = 2


def draw_queries(key, part):
    base = jnp.clip(jax.random.normal(key, (L, HD), jnp.float32), -5.0, 5.0)
    return base.astype(jnp.bfloat16)


def draw_valid_count(key, part):
    first_key = jax.random.fold_in(key, 11)
    second_key = jax.random.fold_in(key, 23)
    counts = jax.random.randint(first_key, (SLIDES,), TILES // 4, TILES + 1, dtype=jnp.int32)
    chosen = jax.random.randint(second_key, (), 0, SLIDES, dtype=jnp.int32)
    return jnp.where(jnp.arange(SLIDES, dtype=jnp.int32) == chosen, jnp.int32(TILES), counts)


def touch_ends(array, rng, smallest, largest):
    shape = array.shape
    index_at = [jax.random.randint(jax.random.fold_in(rng, axis), (), 0, shape[axis]) for axis in range(len(shape))]
    array = array.at[tuple(index_at)].set(smallest)
    longest = shape.index(max(shape))
    index_at[longest] = (index_at[longest] + 1) % shape[longest]
    return array.at[tuple(index_at)].set(largest)


def steps_of(rng, dims, split, least, largest):
    loudness = 1.0
    for dim, blocks in split:
        draws = jax.random.uniform(jax.random.fold_in(jax.random.fold_in(rng, 6), dim), (blocks,), jnp.float32, least / len(split), largest / len(split))
        loudness = loudness * jnp.repeat(jnp.exp(draws), dims[dim] // blocks).reshape((-1,) + (1,) * (len(dims) - 1 - dim))
    return loudness


def normal_values(rng, extent, width, most, cuts=(), held_as=jnp.bfloat16):
    values = width * jax.random.normal(rng, extent, jnp.float32)
    if cuts:
        values = values * steps_of(rng, extent, cuts, -0.22, 0.18)
    return jnp.clip(values, -most, most).astype(held_as)


def setup_inputs(seed: int = 0) -> dict:
    arg_keys = jax.random.split(jax.random.key(seed), 8)
    return {
        "tiles_in": normal_values(arg_keys[0], (SLIDES, TILES, DX), 1.0, 6.0, ((0, 4), (1, 64))),
        "key_weight": normal_values(arg_keys[1], (DX, HD), DX ** -0.5, 0.125, ((0, 64), (1, 2))),
        "value_weight": normal_values(arg_keys[2], (DX, HD), DX ** -0.5, 0.125, ((0, 64), (1, 2))),
        "queries": draw_queries(jax.random.fold_in(arg_keys[7], 71), 0),
        "out_grad": normal_values(arg_keys[4], (SLIDES, L, HD), (TILES / 64), 1536.0, ((0, 4), (2, 2))),
        "valid_count": draw_valid_count(jax.random.fold_in(arg_keys[7], 71), 0),
        "tile_mask": touch_ends((jax.random.randint(arg_keys[6], (SLIDES, TILES), 0, 8) < 7).astype(jnp.int32), jax.random.fold_in(arg_keys[6], 1), 0, 1),
    }


NEG_LARGE = -1e30


def one_slide(tiles_one, grad_one, count_one, mask_one, key_weight, value_weight, queries):
    inv_scale = HDIM ** -0.5
    keys = jnp.dot(tiles_one, key_weight, preferred_element_type=jnp.float32)
    values = jnp.dot(tiles_one, value_weight, preferred_element_type=jnp.float32).astype(jnp.bfloat16)
    positions = jnp.arange(TILES, dtype=jnp.int32)
    valid = ((positions < count_one) & ((mask_one == 1) | (positions == 0)))[None, :]
    queries_wide = queries.astype(jnp.float32)

    def one_head(head_index):
        first = (head_index * HDIM).astype(jnp.int32)
        zero = jnp.zeros((), jnp.int32)
        query_cols = lax.dynamic_slice(queries, (zero, first), (L, HDIM))
        query_wide = lax.dynamic_slice(queries_wide, (zero, first), (L, HDIM))
        key_cols = lax.dynamic_slice(keys, (zero, first), (TILES, HDIM))
        value_cols = lax.dynamic_slice(values, (zero, first), (TILES, HDIM))
        grad_cols = lax.dynamic_slice(grad_one, (zero, first), (L, HDIM))
        scores = jnp.dot(query_wide, key_cols.T, precision=lax.Precision.HIGHEST, preferred_element_type=jnp.float32) * inv_scale
        row_max = jnp.max(jnp.where(valid, scores, NEG_LARGE), axis=1)
        expd = jnp.where(valid, jnp.exp(scores - row_max[:, None]), 0.0)
        total = jnp.sum(expd, axis=1)
        prob_grad = jnp.dot(grad_cols, value_cols.T, preferred_element_type=jnp.float32)
        delta = jnp.sum(expd * prob_grad, axis=1) / total
        probs = expd / total[:, None]
        dscore = (inv_scale * probs * (prob_grad - delta[:, None])).astype(jnp.bfloat16)
        value_grad = jnp.dot(probs.astype(jnp.bfloat16).T, grad_cols, preferred_element_type=jnp.float32).astype(jnp.bfloat16)
        key_grad = jnp.dot(dscore.T, query_cols, preferred_element_type=jnp.float32).astype(jnp.bfloat16)
        return key_grad, value_grad

    key_grad, value_grad = lax.map(one_head, jnp.arange(HEADS, dtype=jnp.int32))
    key_grad = jnp.transpose(key_grad, (1, 0, 2)).reshape(TILES, HD)
    value_grad = jnp.transpose(value_grad, (1, 0, 2)).reshape(TILES, HD)
    group_width = HD // N_HEAD
    summed = jnp.zeros((TILES, DX), jnp.float32)
    for group in range(N_HEAD):
        lower = group * group_width
        upper = lower + group_width
        partial_sum = jnp.dot(key_grad[:, lower:upper], key_weight[:, lower:upper].T, preferred_element_type=jnp.float32)
        partial_sum = partial_sum + jnp.dot(value_grad[:, lower:upper], value_weight[:, lower:upper].T, preferred_element_type=jnp.float32)
        rounded = lax.optimization_barrier(partial_sum.astype(jnp.bfloat16))
        summed = summed + rounded.astype(jnp.float32)
    return summed.astype(jnp.bfloat16)


def reference(tiles_in, key_weight, value_weight, queries, out_grad, valid_count, tile_mask):
    results = []
    for slide in range(SLIDES):
        results.append(one_slide(tiles_in[slide], out_grad[slide], valid_count[slide], tile_mask[slide], key_weight, value_weight, queries))
    return jnp.stack(results, axis=0)
```

```python
import jax
import jax.numpy as jnp
from jax import lax
from jax.sharding import Mesh
from jax.sharding import PartitionSpec as P

HDIM = 80
X_CHIPS = 4
NEG_LARGE = -1e30
SWAP = [(0, 1), (1, 0)]


def spread(value, axis, size):
    copies = jnp.broadcast_to(value[None], (size,) + value.shape)
    return lax.all_to_all(copies, axis, 0, 0, tiled=True)


def merge(stats, new_max):
    scale = jnp.exp(stats[:, 0] - new_max[None])
    return jnp.stack([new_max, jnp.sum(stats[:, 1] * scale, 0), jnp.sum(stats[:, 2] * scale, 0)])


def make_per_device(n_dp, n_zh, n_zl, n_x):
    def per_device(tiles_in, key_weight, value_weight, queries, out_grad, valid_count, tile_mask):
        inv_scale = HDIM ** (-0.5)
        tile_dev, width = tiles_in.shape[1:]
        latents, group = queries.shape
        rows = key_weight.shape[0]
        cols = group // n_x
        heads = cols // HDIM
        z = ("zh", "zl")
        core = lax.axis_index("head")
        plane = lax.axis_index("dp")
        mine = lax.axis_index("x")
        half = tile_dev // 2

        positions = (lax.axis_index(z) * n_x + mine) * tile_dev + jnp.arange(tile_dev, dtype=jnp.int32)
        kept = (tile_mask[0] == 1) | (positions == 0)
        valid = ((positions < valid_count[0]) & kept).astype(jnp.bfloat16)

        own_rows = lax.dynamic_slice(tiles_in[0], (core * half, 0), (half, width))
        own_tiles = lax.all_gather(own_rows, "x", axis=0, tiled=True)

        blocks = jnp.concatenate(
            [key_weight.reshape(rows, n_x, cols), value_weight.reshape(rows, n_x, cols)], axis=2
        ).transpose(1, 0, 2)
        flags = jnp.broadcast_to(
            jnp.pad(valid, (0, 2 * cols - tile_dev))[None, None], (n_x, 8, 2 * cols)
        )
        got = lax.all_to_all(jnp.concatenate([blocks, flags], axis=1), "x", 0, 0, tiled=True)
        flags = got[:, rows, :tile_dev]
        block = lax.dynamic_index_in_dim(got, plane, 0, keepdims=False)[:rows]
        plane_rows = lax.all_gather(block, z, axis=0, tiled=True)
        own_tiles, plane_rows = lax.optimization_barrier((own_tiles, plane_rows))
        other_tiles = lax.ppermute(own_tiles, "head", SWAP)
        weights = spread(plane_rows, "dp", n_dp)
        weights = weights.reshape(n_x, n_zh * n_zl, rows, 2 * cols).transpose(1, 0, 2, 3)
        weights = weights.reshape(width, 2 * cols)
        out_half = width // 2
        other_weights = lax.ppermute(
            lax.dynamic_slice(weights, ((1 - core) * out_half, 0), (out_half, 2 * cols)), "head", SWAP
        )
        own_weights = lax.dynamic_slice(weights, (core * out_half, 0), (out_half, 2 * cols))

        flags = flags.reshape(n_x, 2, half)
        order = jnp.stack([core, 1 - core])
        flags = jnp.take(flags, order, axis=1).transpose(1, 0, 2).reshape(-1)
        valid = (flags > 0.5)[None, :, None]

        tiles = jnp.concatenate([own_tiles, other_tiles], axis=0)
        tokens = tiles.shape[0]
        both = jnp.dot(tiles, weights, preferred_element_type=jnp.float32)
        keys = both[:, :cols].reshape(tokens, heads, HDIM)
        values = both[:, cols:].astype(jnp.bfloat16).reshape(tokens, heads, HDIM)
        query_heads = lax.dynamic_slice(queries, (0, mine * cols), (latents, cols)).reshape(latents, heads, HDIM)
        grad_heads = lax.dynamic_slice(out_grad[0], (0, mine * cols), (latents, cols)).reshape(latents, heads, HDIM)
        scores = (
            jnp.einsum(
                "thd,lhd->htl",
                keys,
                query_heads.astype(jnp.float32),
                precision=lax.Precision.HIGHEST,
                preferred_element_type=jnp.float32,
            )
            * inv_scale
        )
        prob_grad = jnp.einsum("thd,lhd->htl", values, grad_heads, preferred_element_type=jnp.float32)
        local_max = jnp.max(jnp.where(valid, scores, NEG_LARGE), axis=1)
        expd = jnp.where(valid, jnp.exp(scores - local_max[:, None]), 0.0)
        stats = jnp.stack([local_max, jnp.sum(expd, axis=1), jnp.sum(expd * prob_grad, axis=1)])
        for axis, size in (("zl", n_zl), ("zh", n_zh)):
            parts = spread(stats, axis, size)
            stats = merge(parts, jnp.max(parts[:, 0], axis=0))
        row_max, total, weighted = stats
        factor = jnp.exp(local_max - row_max) / total
        delta = weighted / total
        probs = expd * factor[:, None]
        dscore = (inv_scale * probs * (prob_grad - delta[:, None])).astype(jnp.bfloat16)
        value_grad = jnp.einsum(
            "htl,lhd->thd", probs.astype(jnp.bfloat16), grad_heads, preferred_element_type=jnp.float32
        )
        key_grad = jnp.einsum("htl,lhd->thd", dscore, query_heads, preferred_element_type=jnp.float32)
        grads = jnp.concatenate(
            [key_grad.reshape(tokens, cols), value_grad.reshape(tokens, cols)], axis=1
        ).astype(jnp.bfloat16)
        other_grads = lax.ppermute(grads, "head", SWAP)
        other_grads = jnp.concatenate([other_grads[tokens // 2 :], other_grads[: tokens // 2]], axis=0)
        dims = (((1,), (1,)), ((), ()))
        partial = lax.dot_general(grads, own_weights, dims, preferred_element_type=jnp.float32)
        partial = partial + lax.dot_general(other_grads, other_weights, dims, preferred_element_type=jnp.float32)
        partial = partial.astype(jnp.bfloat16).reshape(2, n_x, half, out_half).transpose(1, 0, 2, 3)
        parts = lax.all_to_all(partial, "x", 0, 0, tiled=True)
        summed = jnp.sum(parts.astype(jnp.float32), axis=0).astype(jnp.bfloat16)
        summed = jnp.where(core == 0, summed, summed[::-1])
        return summed.reshape(1, tile_dev, out_half)

    return per_device


def solution(mesh):
    n_dp, n_head, n_tile = mesh.devices.shape
    n_z = n_tile // X_CHIPS
    n_zl = 4
    fine = Mesh(
        mesh.devices.reshape(n_dp, n_head, n_z // n_zl, n_zl, X_CHIPS), ("dp", "head", "zh", "zl", "x")
    )
    tile = ("zh", "zl", "x")
    return jax.shard_map(
        make_per_device(n_dp, n_z // n_zl, n_zl, X_CHIPS),
        mesh=fine,
        in_specs=(
            P("dp", tile, None),
            P(tile, "head"),
            P(tile, "head"),
            P(None, "head"),
            P("dp", None, "head"),
            P("dp"),
            P("dp", tile),
        ),
        out_specs=P("dp", tile, "head"),
        check_vma=False,
    )
```
